32 devices in a mesh: ctx: 16 (over z, x, core), cand: 2 (over y).
Axes of the slice: x: 2, y: 2, z: 4, core: 2. Of those that a mesh axis runs over, the one named last changes fastest.
Arguments:
- queries: bfloat16 [512, 1024], P(('cand', 'ctx')), may hold values from -256 to 256
- grad_out: bfloat16 [512, 1024], P(('cand', 'ctx')), may hold values from -6 to 6
- prefix_keys: bfloat16 [16384, 128], P(('ctx', 'cand')), may hold values from -4 to 4
- prefix_values: bfloat16 [16384, 128], P(('ctx', 'cand')), may hold values from -6 to 6
- cand_keys: bfloat16 [512, 128], P('cand'), may hold values from -6 to 6
- cand_values: bfloat16 [512, 128], P('cand'), may hold values from -6 to 6
- lengths: int32 [2, 4], P('cand'), may hold values from 1 to 128, 256 in all within a row
- offsets: int32 [8], P('cand'), may hold values from 4096 to 16384
Outputs:
- grad_queries: bfloat16 [512, 1024], P(('cand', 'ctx'))
- grad_keys: bfloat16 [16384, 128], P(('ctx', 'cand'))
- grad_values: bfloat16 [16384, 128], P(('ctx', 'cand'))
The draws below stay inside these ranges and needn't reach their ends.
Inputs may be any that keep to these rules, and one draw needn't show every extreme that they name: Each row of lengths sums to 256.
All inputs are finite; a program needn't handle non-finite values.
Results may differ from the reference program's by a relative error of at most 0.015.
Values may be sent and summed in bfloat16 or wider, within the bound.
No kernel may reach another device: no remote copies, remote signals or barrier semaphores. Data moves between devices by JAX's collectives and lax.ppermute only.
A program may use at most 64 MiB of HBM per device.

```python
import math
import jax
import jax.numpy as jnp
import numpy as np
from jax import lax

HEADS = 8
HD = 128
C_BLK = 256
S_BLK = 4
PREFIX = 16384
CAND = 512
SAMPLES = 8
N_CAND = 2


def base_keys(key):
    return jnp.clip(jax.random.normal(jax.random.fold_in(key, 11), (PREFIX, HD), jnp.float32), -4.0, 4.0)


def draw_prefix_keys(key, part):
    keys_base = base_keys(key)
    return keys_base.astype(jnp.bfloat16)


def draw_queries(key, part):
    drawn = jnp.clip(jax.random.normal(jax.random.fold_in(key, 23), (CAND, HEADS * HD), jnp.float32), -4.0, 4.0)
    return drawn.astype(jnp.bfloat16)


def set_ends(values, stream_key, low, largest):
    shape = values.shape
    place = [jax.random.randint(jax.random.fold_in(stream_key, axis), (), 0, shape[axis]) for axis in range(len(shape))]
    values = values.at[tuple(place)].set(low)
    longest = shape.index(max(shape))
    place[longest] = (place[longest] + 1) % shape[longest]
    return values.at[tuple(place)].set(largest)


def shard_levels(stream_key, extent, pieces, low, high):
    factor_of = 1.0
    for dim, parts in pieces:
        draws = jax.random.uniform(jax.random.fold_in(jax.random.fold_in(stream_key, 6), dim), (parts,), jnp.float32, low / len(pieces), high / len(pieces))
        factor_of = factor_of * jnp.repeat(jnp.exp(draws), extent[dim] // parts).reshape((-1,) + (1,) * (len(extent) - 1 - dim))
    return factor_of


def split_up(count, total, bound, lean):
    weights = [(1 << 20) // math.isqrt(standing ** lean) + 1 for standing in range(2, count + 1)]
    rest, given = total - bound - (count - 1), [1] * (count - 1)
    while rest > 0:
        movable = [i for i in range(count - 1) if given[i] < bound]
        whole, budget = sum([weights[i] for i in movable]), rest
        for i in movable:
            addition = min(bound - given[i], max(1, budget * weights[i] // whole), rest)
            given[i] = given[i] + addition
            rest = rest - addition
    return np.array([bound] + given)


def uneven_parts(rng, amount, total, bound, lean):
    if amount == 2:
        one = jax.random.randint(rng, (), max(1, total - bound), min(bound, total - 1) + 1)
        return jnp.stack([one, total - one])
    sizes = jnp.asarray(split_up(amount, total, bound, lean), jnp.int32)
    couples = (amount - 1) // 2
    giver, taker = sizes[1:1 + 2 * couples:2], sizes[2:2 + 2 * couples:2]
    slack = jnp.minimum(giver - 1, bound - taker)
    passed = jax.random.randint(jax.random.fold_in(rng, 1), (couples,), 0, 1 << 20) % (slack + 1)
    sizes = sizes.at[1:1 + 2 * couples:2].set(giver - passed).at[2:2 + 2 * couples:2].set(taker + passed)
    return sizes[jax.random.permutation(jax.random.fold_in(rng, 2), amount)]


def scatter_about(key, shape, spread, most, pieces=(), kind=jnp.bfloat16):
    result = spread * jax.random.normal(key, shape, jnp.float32)
    if pieces:
        result = result * shard_levels(key, shape, pieces, -0.22, 0.18)
    return jnp.clip(result, -most, most).astype(kind)


def setup_inputs(seed: int = 0) -> dict:
    splits = jax.random.split(jax.random.key(seed), 9)
    return {
        "queries": draw_queries(jax.random.fold_in(splits[8], 71), 0),
        "grad_out": scatter_about(splits[1], (CAND, HEADS * HD), 1.0, 6.0, ((0, 32),)),
        "prefix_keys": draw_prefix_keys(jax.random.fold_in(splits[8], 71), 0),
        "prefix_values": scatter_about(splits[3], (PREFIX, HD), 1.0, 6.0, ((0, 32),)),
        "cand_keys": scatter_about(splits[4], (CAND, HD), 1.0, 6.0, ((0, 2),)),
        "cand_values": scatter_about(splits[5], (CAND, HD), 1.0, 6.0, ((0, 2),)),
        "lengths": jax.vmap(lambda own: uneven_parts(own, S_BLK, C_BLK, C_BLK // 2, 2))(jax.random.split(splits[6], N_CAND)).reshape((N_CAND, S_BLK)).astype(jnp.int32),
        "offsets": set_ends(jax.random.randint(splits[7], (SAMPLES,), PREFIX // 4, PREFIX + 1), jax.random.fold_in(splits[7], 1), PREFIX // 4, PREFIX).astype(jnp.int32),
    }


NEG = -1e+30

def sample_rows(lengths, offsets):
    ends = jnp.cumsum(lengths, axis=1).astype(jnp.int32)
    local = jnp.arange(C_BLK, dtype=jnp.int32)
    segment = lax.optimization_barrier(jnp.sum((local[None, :, None] >= ends[:, None, :]).astype(jnp.int32), axis=2)).astype(jnp.int32)
    owner = (segment + (jnp.arange(N_CAND, dtype=jnp.int32) * S_BLK)[:, None]).astype(jnp.int32)
    limit = jnp.take(offsets, owner.reshape(-1)).reshape(N_CAND, C_BLK).astype(jnp.int32)
    return (segment, limit)

def reference(queries, grad_out, prefix_keys, prefix_values, cand_keys, cand_values, lengths, offsets):
    scaling = 1.0 / math.sqrt(HD)
    segment, limit = sample_rows(lengths, offsets)
    position = jnp.arange(PREFIX, dtype=jnp.int32)
    local = jnp.arange(C_BLK, dtype=jnp.int32)
    values_wide = prefix_values.astype(jnp.float32)
    query_heads = queries.reshape(N_CAND, C_BLK, HEADS, HD).transpose(0, 2, 1, 3)
    grad_heads = grad_out.reshape(N_CAND, C_BLK, HEADS, HD).transpose(0, 2, 1, 3)
    block_keys = cand_keys.reshape(N_CAND, C_BLK, HD)
    block_values = cand_values.reshape(N_CAND, C_BLK, HD)

    def one_block(carry, bundle):
        query_set, grad_set, own_keys, own_values, seg_block, limit_block = bundle
        seen = position[None, :] < limit_block[:, None]
        mine = (seg_block[:, None] == seg_block[None, :]) & (local[None, :] <= local[:, None])

        def one_head(pair):
            query, upstream = pair
            score_pre = jnp.dot(query, prefix_keys.T, preferred_element_type=jnp.float32) * scaling
            score_own = jnp.dot(query, own_keys.T, preferred_element_type=jnp.float32) * scaling
            highest = jnp.maximum(lax.optimization_barrier(jnp.max(jnp.where(seen, score_pre, NEG), axis=1)), lax.optimization_barrier(jnp.max(jnp.where(mine, score_own, NEG), axis=1)))
            exp_pre = jnp.where(seen, jnp.exp(score_pre - highest[:, None]), 0.0)
            exp_own = jnp.where(mine, jnp.exp(score_own - highest[:, None]), 0.0)
            totals = lax.optimization_barrier(jnp.sum(exp_pre, axis=1)) + lax.optimization_barrier(jnp.sum(exp_own, axis=1))
            prob_pre = exp_pre / totals[:, None]
            prob_own = exp_own / totals[:, None]
            output = jnp.dot(prob_pre, values_wide, precision=lax.Precision.HIGHEST, preferred_element_type=jnp.float32)
            output = output + jnp.dot(prob_own, own_values.astype(jnp.float32), precision=lax.Precision.HIGHEST, preferred_element_type=jnp.float32)
            delta = lax.optimization_barrier(jnp.sum(upstream.astype(jnp.float32) * output, axis=1))
            prod_pre = jnp.dot(upstream, prefix_values.T, preferred_element_type=jnp.float32)
            prod_own = jnp.dot(upstream, own_values.T, preferred_element_type=jnp.float32)
            slope_pre = (prob_pre * (prod_pre - delta[:, None])).astype(jnp.bfloat16)
            slope_own = (prob_own * (prod_own - delta[:, None])).astype(jnp.bfloat16)
            grad_query = scaling * (jnp.dot(slope_pre, prefix_keys, preferred_element_type=jnp.float32) + jnp.dot(slope_own, own_keys, preferred_element_type=jnp.float32))
            grad_key = scaling * jnp.dot(slope_pre.T, query, preferred_element_type=jnp.float32)
            grad_value = jnp.dot(prob_pre.astype(jnp.bfloat16).T, upstream, preferred_element_type=jnp.float32)
            return (grad_query, grad_key, grad_value)
        grad_query, grad_key, grad_value = lax.map(one_head, (query_set, grad_set))
        carry = (carry[0] + lax.optimization_barrier(jnp.sum(grad_key, axis=0)), carry[1] + lax.optimization_barrier(jnp.sum(grad_value, axis=0)))
        return (carry, grad_query)
    start = (jnp.zeros((PREFIX, HD), jnp.float32), jnp.zeros((PREFIX, HD), jnp.float32))
    (key_total, value_total), grad_query = lax.scan(one_block, start, (query_heads, grad_heads, block_keys, block_values, segment, limit))
    grad_queries = grad_query.transpose(0, 2, 1, 3).reshape(CAND, HEADS * HD).astype(jnp.bfloat16)
    return (grad_queries, key_total.astype(jnp.bfloat16), value_total.astype(jnp.bfloat16))
```

```python
import functools
import itertools
import math

import jax
import jax.numpy as jnp
from jax import lax
from jax.experimental import pallas as pl
from jax.experimental.pallas import tpu as pltpu
from jax.sharding import PartitionSpec as P

HEADS = 8
HD = 128
NEG = -1e30
SCALING = 1.0 / math.sqrt(HD)
RATE = SCALING * math.log2(math.e)
BOTH = ("ctx", "cand")
NT = (((1,), (1,)), ((), ()))
TN = (((0,), (0,)), ((), ()))


class Layout:
    def __init__(self, mesh):
        ctx, self.cand = mesh.shape["ctx"], mesh.shape["cand"]
        self.core = 2
        self.x = 2
        self.z = ctx // (self.core * self.x)

    def linear(self, z, x, core, cand):
        return ((z * self.x + x) * self.core + core) * self.cand + cand

    def permute(self, array, dz=0, dx=0, dcore=0, dcand=0):
        places = itertools.product(*map(range, (self.z, self.x, self.core, self.cand)))
        pairs = [
            (self.linear(z, x, c, y), self.linear(z ^ dz, x ^ dx, c ^ dcore, y ^ dcand))
            for z, x, c, y in places
        ]
        return lax.ppermute(array, BOTH, pairs)

    def key_steps(self):
        return [(dx, dy) for dx in range(self.x) for dy in range(self.cand)]

    def here(self):
        ctx, cand = lax.axis_index("ctx"), lax.axis_index("cand")
        core = ctx % self.core
        x = (ctx // self.core) % self.x
        z = ctx // (self.core * self.x)
        return z, x, core, cand


def token_limits(layout, owned, here, lengths_ref, offsets_ref):
    z, x, core, _ = here
    tokens = layout.z * layout.core * owned
    lane = lax.broadcasted_iota(jnp.int32, (1, tokens), 1)
    half = lane // (layout.z * owned)
    slot = (lane // owned) % layout.z
    place = ((jnp.bitwise_xor(slot, z) * layout.x + x) * layout.core) + jnp.bitwise_xor(half, core)
    pos = place * owned + lane % owned
    limit = jnp.full((1, tokens), offsets_ref[0], jnp.int32)
    start = jnp.zeros((1, tokens), jnp.int32)
    end = jnp.int32(0)
    for b in range(1, lengths_ref.shape[1]):
        end = end + lengths_ref[0, b - 1]
        later = pos >= end
        limit = jnp.where(later, offsets_ref[b], limit)
        start = jnp.where(later, end, start)
    return limit, start, pos


def pair(vector):
    return jnp.concatenate([vector, vector], axis=1)


def swap_lanes(vector, amount):
    lanes = vector.shape[-1]
    lane = lax.broadcasted_iota(jnp.int32, vector.shape, vector.ndim - 1)
    axis = vector.ndim - 1
    down = pltpu.roll(vector, lanes - amount, axis)
    if 2 * amount == lanes:
        return down
    return jnp.where((lane // amount) % 2 == 0, down, pltpu.roll(vector, amount, axis))


def rows_of(half_a, half_b, q_rows, g_rows):
    tokens = half_a.shape[0]
    for h in range(HEADS):
        lanes = slice(h * HD, (h + 1) * HD)
        upper = slice((HEADS + h) * HD, (HEADS + h + 1) * HD)
        for k, half in enumerate((half_a, half_b)):
            rows = slice(h * 2 * tokens + k * tokens, h * 2 * tokens + (k + 1) * tokens)
            q_rows[rows, :] = half[:, lanes]
            g_rows[rows, :] = half[:, upper]


def key_blocks(layout, here, key_refs, cand_keys, cand_values, limits):
    z, x, core, cand = here
    limit, start, pos = limits
    wide = 2 * limit.shape[1]
    limit2, start2, pos2 = pair(limit), pair(start), pair(pos)
    for (dx, dy), ref in zip(layout.key_steps(), key_refs):
        count = ref.shape[1]
        base = layout.linear(z, jnp.bitwise_xor(x, dx), core, jnp.bitwise_xor(cand, dy)) * count

        def visible(count=count, base=base):
            index = lax.broadcasted_iota(jnp.int32, (count, wide), 0)
            return index < (limit2 - base)

        yield ref[0], ref[1], visible
    count = cand_keys.shape[0] // (layout.z * layout.core)
    first = pl.multiple_of((z * layout.core + core) * count, count)

    def allowed():
        index = lax.broadcasted_iota(jnp.int32, (count, wide), 0) + first
        return (index >= start2) & (index <= pos2)

    yield cand_keys[pl.ds(first, count), :], cand_values[pl.ds(first, count), :], allowed


def forward_kernel(layout, owned, steps, *refs):
    lengths_ref, offsets_ref, half_a, half_b = refs[:4]
    key_refs, (cand_keys, cand_values) = refs[4 : 4 + steps], refs[4 + steps : 6 + steps]
    stats, stats_turned, q_rows, g_rows = refs[6 + steps :]
    here = layout.here()
    rows_of(half_a, half_b, q_rows, g_rows)
    limits = token_limits(layout, owned, here, lengths_ref, offsets_ref)
    tokens = limits[0].shape[1]
    total = [None] * (HEADS // 2)
    for keys, values, visible in key_blocks(layout, here, key_refs, cand_keys, cand_values, limits):
        seen = visible()
        for p in range(HEADS // 2):
            rows = slice(p * 2 * tokens, (p + 1) * 2 * tokens)
            scores = lax.dot_general(keys, q_rows[rows, :], NT, preferred_element_type=jnp.float32)
            products = lax.dot_general(values, g_rows[rows, :], NT, preferred_element_type=jnp.float32)
            scores = jnp.where(seen, scores, NEG)
            high = jnp.max(scores, axis=0, keepdims=True)
            if total[p] is not None:
                high = jnp.maximum(high, total[p][0])
            expon = jnp.exp2((scores - high) * RATE)
            mass = jnp.sum(expon, axis=0, keepdims=True)
            carry = jnp.sum(expon * products, axis=0, keepdims=True)
            if total[p] is not None:
                fade = jnp.exp2((total[p][0] - high) * RATE)
                mass = mass + fade * total[p][1]
                carry = carry + fade * total[p][2]
            total[p] = (high, mass, carry)
    for p in range(HEADS // 2):
        high, mass, carry = total[p]
        none = high <= NEG
        mass = jnp.where(none, 0.0, mass)
        carry = jnp.where(none, 0.0, carry)
        for k, value in enumerate((high, mass, carry)):
            stats[k, 2 * p : 2 * p + 1, :] = value[:, :tokens]
            stats[k, 2 * p + 1 : 2 * p + 2, :] = value[:, tokens:]
    for k in range(3):
        stats_turned[k] = swap_lanes(stats[k], tokens // 2)


def joined(parts):
    high = functools.reduce(jnp.maximum, [p[0] for p in parts])
    fades = [jnp.exp2((p[0] - high) * RATE) for p in parts]
    mass = sum(p[1] * f for p, f in zip(parts, fades))
    carry = sum(p[2] * f for p, f in zip(parts, fades))
    return high, mass, carry


def backward_kernel(layout, owned, steps, *refs):
    lengths_ref, offsets_ref, q_rows, g_rows = refs[:4]
    stat_refs = refs[4 : 4 + layout.z]
    at = 4 + layout.z
    key_refs, (cand_keys, cand_values) = refs[at : at + steps], refs[at + steps : at + steps + 2]
    at = at + steps + 2
    outs, (dq_own, dq_other) = refs[at : at + steps], refs[at + steps : at + steps + 2]
    probs, slopes, all_keys = refs[at + steps + 2 :]
    here = layout.here()
    limits = token_limits(layout, owned, here, lengths_ref, offsets_ref)
    tokens = limits[0].shape[1]
    parts = []
    for d, ref in enumerate(stat_refs):
        part = [ref[k] for k in range(3)]
        for bit in range(layout.z.bit_length()):
            if d >> bit & 1:
                part = [swap_lanes(value, owned << bit) for value in part]
        parts.append(part)
    high, mass, carry = joined(parts)
    shift = high + jnp.log2(mass) * (1.0 / RATE)
    delta = carry / mass

    def lanes_of(vector, p):
        return jnp.concatenate([vector[2 * p : 2 * p + 1], vector[2 * p + 1 : 2 * p + 2]], axis=1)

    done = 0
    blocks = key_blocks(layout, here, key_refs, cand_keys, cand_values, limits)
    for i, (keys, values, visible) in enumerate(blocks):
        count = keys.shape[0]
        seen = visible()
        all_keys[done : done + count, :] = keys
        for p in range(HEADS // 2):
            rows = slice(p * 2 * tokens, (p + 1) * 2 * tokens)
            scores = lax.dot_general(keys, q_rows[rows, :], NT, preferred_element_type=jnp.float32)
            products = lax.dot_general(values, g_rows[rows, :], NT, preferred_element_type=jnp.float32)
            scores = jnp.where(seen, scores, NEG)
            prob = jnp.exp2((scores - lanes_of(shift, p)) * RATE)
            slope = prob * (products - lanes_of(delta, p))
            slopes[done : done + count, rows] = slope.astype(jnp.bfloat16)
            if i < steps:
                probs[:, rows] = prob.astype(jnp.bfloat16)
        if i < steps:
            key_part = jnp.dot(
                slopes[done : done + count, :], q_rows[...], preferred_element_type=jnp.float32
            )
            value_part = jnp.dot(probs[...], g_rows[...], preferred_element_type=jnp.float32)
            outs[i][0] = (SCALING * key_part).astype(outs[i].dtype)
            outs[i][1] = value_part.astype(outs[i].dtype)
        done += count
    turned = lax.dot_general(all_keys[...], slopes[...], TN, preferred_element_type=jnp.float32)
    half = tokens // 2
    for h in range(HEADS):
        block = SCALING * jnp.transpose(turned[:, h * tokens : (h + 1) * tokens])
        dq_own[:, h * HD : (h + 1) * HD] = block[:half]
        dq_other[:, h * HD : (h + 1) * HD] = block[half:].astype(jnp.bfloat16)


def body(layout, queries, grad_out, prefix_keys, prefix_values, cand_keys, cand_values, lengths, offsets):
    owned = queries.shape[0]
    count = prefix_keys.shape[0]
    steps = layout.key_steps()
    pairs = jnp.stack([prefix_keys, prefix_values])
    key_sets = [pairs] + [layout.permute(pairs, dx=dx, dcand=dy) for dx, dy in steps[1:]]
    mine = jnp.concatenate([queries, grad_out], axis=1)
    half_a = jnp.concatenate([mine] + [layout.permute(mine, dz=d) for d in range(1, layout.z)], axis=0)
    half_b = layout.permute(half_a, dcore=1)
    tokens = 2 * half_a.shape[0]
    rows = tokens * HEADS
    vmem = pl.BlockSpec(memory_space=pltpu.VMEM)
    smem = pl.BlockSpec(memory_space=pltpu.SMEM)
    params = pltpu.CompilerParams(vmem_limit_bytes=40 * 1024 * 1024)
    stats, turned, q_rows, g_rows = pl.pallas_call(
        functools.partial(forward_kernel, layout, owned, len(steps)),
        out_shape=(
            jax.ShapeDtypeStruct((3, HEADS, tokens), jnp.float32),
            jax.ShapeDtypeStruct((3, HEADS, tokens), jnp.float32),
            jax.ShapeDtypeStruct((rows, HD), jnp.bfloat16),
            jax.ShapeDtypeStruct((rows, HD), jnp.bfloat16),
        ),
        in_specs=[smem, smem] + [vmem] * (4 + len(steps)),
        out_specs=(vmem,) * 4,
        compiler_params=params,
        name="forward",
    )(lengths, offsets, half_a, half_b, *key_sets, cand_keys, cand_values)
    stats = jnp.stack(joined([stats, layout.permute(turned, dcore=1)]))
    all_stats = [stats] + [layout.permute(stats, dz=d) for d in range(1, layout.z)]
    total_keys = count * len(steps) + cand_keys.shape[0] // (layout.z * layout.core)
    outs = pl.pallas_call(
        functools.partial(backward_kernel, layout, owned, len(steps)),
        out_shape=(
            [jax.ShapeDtypeStruct((2, count, HD), jnp.float32)]
            + [jax.ShapeDtypeStruct((2, count, HD), jnp.bfloat16)] * (len(steps) - 1)
            + [
                jax.ShapeDtypeStruct((tokens // 2, HEADS * HD), jnp.float32),
                jax.ShapeDtypeStruct((tokens // 2, HEADS * HD), jnp.bfloat16),
            ]
        ),
        in_specs=[smem, smem] + [vmem] * (4 + layout.z + len(steps)),
        out_specs=[vmem] * (len(steps) + 2),
        scratch_shapes=[
            pltpu.VMEM((count, rows), jnp.bfloat16),
            pltpu.VMEM((total_keys, rows), jnp.bfloat16),
            pltpu.VMEM((total_keys, HD), jnp.bfloat16),
        ],
        compiler_params=params,
        name="backward",
    )(lengths, offsets, q_rows, g_rows, *all_stats, *key_sets, cand_keys, cand_values)
    key_parts, (dq_own, dq_other) = outs[: len(steps)], outs[len(steps) :]
    key_value_grads = key_parts[0]
    for (dx, dy), part in zip(steps[1:], key_parts[1:]):
        key_value_grads = key_value_grads + layout.permute(part, dx=dx, dcand=dy).astype(jnp.float32)
    dq = dq_own + layout.permute(dq_other, dcore=1).astype(jnp.float32)
    grad_queries = dq[:owned]
    for d in range(1, layout.z):
        piece = dq[d * owned : (d + 1) * owned].astype(jnp.bfloat16)
        grad_queries = grad_queries + layout.permute(piece, dz=d).astype(jnp.float32)
    return (
        grad_queries.astype(jnp.bfloat16),
        key_value_grads[0].astype(jnp.bfloat16),
        key_value_grads[1].astype(jnp.bfloat16),
    )


def solution(mesh):
    placed = (
        P(("cand", "ctx"), None),
        P(("cand", "ctx"), None),
        P(("ctx", "cand"), None),
        P(("ctx", "cand"), None),
        P("cand", None),
        P("cand", None),
        P("cand", None),
        P("cand"),
    )
    return jax.shard_map(
        functools.partial(body, Layout(mesh)),
        mesh=mesh,
        in_specs=placed,
        out_specs=(P(("cand", "ctx"), None), P(("ctx", "cand"), None), P(("ctx", "cand"), None)),
        check_vma=False,
    )
```
